32 devices in a mesh: seq: 8 (over y, x, core), tensor: 4 (over z).
Axes of the slice: x: 2, y: 2, z: 4, core: 2. Of those that a mesh axis runs over, the one named last changes fastest.
Arguments:
- patches: bfloat16 [2048, 6144], P('seq', 'tensor'), may hold values from -60 to 60
- segment_ids: int32 [2048], replicated, may hold values from 0 to 3, never falling along the last dimension, each value on 1 to 768 neighbouring positions
- w_query: bfloat16 [6144, 1024], P('seq', 'tensor'), may hold values from -0.078125 to 0.078125
- w_key: bfloat16 [6144, 1024], P('seq', 'tensor'), may hold values from -0.078125 to 0.078125
- w_value: bfloat16 [6144, 1024], P('seq', 'tensor'), may hold values from -0.078125 to 0.078125
- w_out: bfloat16 [1024, 6144], P('seq', 'tensor'), may hold values from -0.1875 to 0.1875
Outputs:
- attended: bfloat16 [2048, 6144], P('seq', 'tensor')
The draws below stay inside these ranges and needn't reach their ends.
Inputs may be any that keep to these rules, and one draw needn't show every extreme that they name: `segment_ids`: image ids never fall along the row; every image holds at most 768 patches and some image exactly that many.
All inputs are finite; a program needn't handle non-finite values.
Results may differ from the reference program's by a relative error of at most 0.012.
The reference program's roundings to bfloat16 on the way count: a program that leaves them out, or rounds other values in their place, can miss the bound.
Values may be sent and summed in bfloat16 or wider, within the bound.
No kernel may reach another device: no remote copies, remote signals or barrier semaphores. Data moves between devices by JAX's collectives and lax.ppermute only.
A program may use at most 64 MiB of HBM per device.

```python
import math
import jax
import jax.numpy as jnp
import numpy as np
from jax import lax

D = 6144
HS = 128
TOK_DEV = 256
SPAN = 3
HEADS = 8
TOKENS = 2048
IMAGES = 4


def draw_patches(key, part):
    first = jax.random.fold_in(key, 0)
    base = jnp.clip(jax.random.normal(first, (TOKENS, D), jnp.float32), -5.0, 5.0)
    return base.astype(jnp.bfloat16)


def block_levels(stream_key, extent, shards, low, largest):
    def one(position, shards_of):
        steps = jax.random.uniform(jax.random.fold_in(jax.random.fold_in(stream_key, 6), position), (shards_of,), jnp.float32, low / len(shards), largest / len(shards))
        return jnp.repeat(jnp.exp(steps), extent[position] // shards_of).reshape((-1,) + (1,) * (len(extent) - position - 1))

    level = one(*shards[0])
    for cut in shards[1:]:
        level = level * one(*cut)
    return level


def length_profile(amount, total, limit, slope):
    weights = [(1 << 20) // math.isqrt(rank ** slope) + 1 for rank in range(2, amount + 1)]
    surplus, counts = total - limit - (amount - 1), [1] * (amount - 1)
    while surplus > 0:
        free = [i for i in range(amount - 1) if counts[i] < limit]
        whole, budget = sum([weights[i] for i in free]), surplus
        for i in free:
            more = min(limit - counts[i], max(1, budget * weights[i] // whole), surplus)
            counts[i] = counts[i] + more
            surplus = surplus - more
    return np.array([limit] + counts)


def ragged(key, amount, total, limit, lean):
    if amount == 2:
        one = jax.random.randint(key, (), max(1, total - limit), min(limit, total - 1) + 1)
        return jnp.stack([one, total - one])
    sizes = jnp.asarray(length_profile(amount, total, limit, lean), jnp.int32)
    couples = (amount - 1) // 2
    source_of, sink = sizes[1:1 + 2 * couples:2], sizes[2:2 + 2 * couples:2]
    margin = jnp.minimum(source_of - 1, limit - sink)
    passed = jax.random.randint(jax.random.fold_in(key, 1), (couples,), 0, 1 << 20) % (margin + 1)
    sizes = sizes.at[1:1 + 2 * couples:2].set(source_of - passed).at[2:2 + 2 * couples:2].set(sink + passed)
    return sizes[jax.random.permutation(jax.random.fold_in(key, 2), amount)]


def noise(stream_key, extent, spread, reach, shards=(), kind=jnp.bfloat16):
    gain = block_levels(stream_key, extent, shards, -0.22, 0.18) if shards else 1.0
    result = jax.random.normal(stream_key, extent, jnp.float32) * spread * gain
    return jnp.minimum(jnp.maximum(result, -reach), reach).astype(kind)


def setup_inputs(seed: int = 0) -> dict:
    streams_of = jax.random.split(jax.random.key(seed), 7)
    patches = draw_patches(jax.random.fold_in(streams_of[6], 71), 0)
    segment_ids = jnp.searchsorted(jnp.cumsum(ragged(streams_of[1], IMAGES, TOKENS, SPAN * TOK_DEV, 2)), jnp.arange(TOKENS), side="right").astype(jnp.int32)
    w_query = noise(streams_of[2], (D, HEADS * HS), D ** -0.5, 0.078125, ((0, 8), (1, 4)))
    w_key = noise(streams_of[3], (D, HEADS * HS), D ** -0.5, 0.078125, ((0, 8), (1, 4)))
    w_value = noise(streams_of[4], (D, HEADS * HS), D ** -0.5, 0.078125, ((0, 8), (1, 4)))
    w_out = noise(streams_of[5], (HEADS * HS, D), (HEADS * HS) ** -0.5, 0.1875, ((0, 8), (1, 4)))
    return dict(patches=patches, segment_ids=segment_ids, w_query=w_query, w_key=w_key, w_value=w_value, w_out=w_out)


def reference(patches, segment_ids, w_query, w_key, w_value, w_out):
    def project(weight):
        flat = jnp.dot(patches, weight, preferred_element_type=jnp.float32).astype(jnp.bfloat16)
        return flat.reshape(TOKENS, HEADS, HS).transpose(1, 0, 2)

    queries = project(w_query)
    keys_all = project(w_key)
    values_all = project(w_value)
    same_image = segment_ids[:, None] == segment_ids[None, :]
    scaling = HS ** -0.5

    def one_head(items):
        q_head, k_head, v_head = items
        scores = jnp.dot(q_head, k_head.T, preferred_element_type=jnp.float32) * scaling
        scores = jnp.where(same_image, scores, -jnp.inf)
        probs = jax.nn.softmax(scores, axis=-1).astype(jnp.bfloat16)
        return jnp.dot(probs, v_head, preferred_element_type=jnp.float32).astype(jnp.bfloat16)

    heads_out = lax.map(one_head, (queries, keys_all, values_all))
    heads_out = heads_out.transpose(1, 0, 2).reshape(TOKENS, HEADS * HS)
    return jnp.dot(heads_out, w_out, preferred_element_type=jnp.float32).astype(jnp.bfloat16)
```

```python
import jax
import jax.numpy as jnp
from jax import lax
from jax.experimental import pallas as pl
from jax.experimental.pallas import tpu as pltpu
from jax.sharding import PartitionSpec as P

HS = 128
NEG = -1e30
BF16 = jnp.bfloat16
F32 = jnp.float32
ANY = pl.BlockSpec(memory_space=pl.ANY)
VMEM = pl.BlockSpec(memory_space=pltpu.VMEM)
SMEM = pl.BlockSpec(memory_space=pltpu.SMEM)


def reversed_bits(value, bits):
    return sum(((value >> k) & 1) << (bits - 1 - k) for k in range(bits))


def chip_at(position, chip, core, bits):
    return chip ^ jnp.where(core == 0, position, reversed_bits(position, bits))


def gather_chips(x, chips):
    bits = chips.bit_length() - 1
    pieces = [x]
    for k in range(bits):
        pairs = [
            (2 * c + j, 2 * (c ^ (1 << (bits - 1 - k if j else k))) + j)
            for c in range(chips)
            for j in range(2)
        ]
        pieces += [lax.ppermute(pieces[q], "seq", pairs) for q in range(1 << k)]
    return pieces


def swap_cores(x, devices):
    return lax.ppermute(x, "seq", [(s, s ^ 1) for s in range(devices)])


def line_gather(x, count):
    below, above = [x], [x]
    for k in range(1, count):
        below.append(lax.ppermute(below[-1], "tensor", [(i, i + 1) for i in range(k - 1, count - 1)]))
        above.append(lax.ppermute(above[-1], "tensor", [(i + 1, i) for i in range(count - k)]))
    return below, above


def place():
    seq = lax.axis_index("seq")
    return seq // 2, seq % 2, lax.axis_index("tensor")


def project_most(chips, count, steps):
    bits = chips.bit_length() - 1

    def kernel(*refs):
        mine, theirs = refs[:chips], refs[chips : 2 * chips]
        xs = refs[2 * chips : 2 * chips + 1 + 2 * steps]
        acc, x_full, w_full, w_sem, x_sem = refs[2 * chips + 1 + 2 * steps :]
        chip, core, at = place()
        rows = mine[0].shape[0]

        def w_copy(block, source):
            to = w_full.at[pl.ds(pl.multiple_of(block * rows, rows), rows)]
            return pltpu.make_async_copy(source, to, w_sem.at[block])

        for p in range(chips):
            w_copy(2 * chip_at(p, chip, core, bits) + core, mine[p]).start()
            w_copy(2 * chip_at(p, chip, 1 - core, bits) + 1 - core, theirs[p]).start()

        def x_copy(block, source):
            return pltpu.make_async_copy(source, x_full.at[block], x_sem.at[block])

        x_copy(at, xs[0]).start()
        for k in range(1, steps + 1):

            @pl.when(at >= k)
            def _():
                x_copy(at - k, xs[k]).start()

            @pl.when(at + k < count)
            def _():
                x_copy(at + k, xs[steps + k]).start()

        acc[...] = jnp.zeros(acc.shape, F32)
        depth = x_full.shape[2]
        per = depth // rows

        def step(block, _):
            for i in range(per):
                w_copy(block * per + i, mine[0]).wait()

            @pl.when(jnp.abs(block - at) <= steps)
            def _():
                x_copy(block, xs[0]).wait()
                w = w_full[pl.ds(pl.multiple_of(block * depth, depth), depth), :]
                acc[...] += jnp.dot(x_full[block], w, preferred_element_type=F32)

            return 0

        lax.fori_loop(0, count, step, 0)

    return kernel


def project_last(chips, count):
    bits = chips.bit_length() - 1

    def kernel(*refs):
        mine, theirs = refs[:chips], refs[chips : 2 * chips]
        acc_in, from_below, from_above, q_keep, kv_keep, q_send, kv_send = refs[2 * chips : 2 * chips + 7]
        acc, x_block, w_block, w_sem, x_sem, acc_sem = refs[2 * chips + 7 :]
        chip, core, at = place()
        rows = mine[0].shape[0]
        get_acc = pltpu.make_async_copy(acc_in, acc, acc_sem)
        get_acc.start()
        edge = (at == 0) | (at == count - 1)

        def w_copy(kind, source):
            return pltpu.make_async_copy(source, w_block.at[pl.ds(pl.multiple_of(kind * rows, rows), rows)], w_sem.at[kind])

        def x_copy(source):
            return pltpu.make_async_copy(source, x_block, x_sem)

        @pl.when(at == 0)
        def _():
            x_copy(from_above).start()

        @pl.when(at == count - 1)
        def _():
            x_copy(from_below).start()

        wanted = jnp.where(at == 0, count - 1, 0)
        for p in range(chips):

            @pl.when(edge & (chip_at(p, chip, core, bits) == wanted))
            def _():
                w_copy(core, mine[p]).start()

            @pl.when(edge & (chip_at(p, chip, 1 - core, bits) == wanted))
            def _():
                w_copy(1 - core, theirs[p]).start()

        get_acc.wait()

        @pl.when(edge)
        def _():
            x_copy(from_below).wait()
            w_copy(0, mine[0]).wait()
            w_copy(1, mine[0]).wait()
            acc[...] += jnp.dot(x_block[...], w_block[...], preferred_element_type=F32)

        half = acc.shape[1] // 2
        first = acc[:, :half].astype(BF16)
        second = acc[:, half:].astype(BF16)
        keep = jnp.where(core == 0, first, second)
        send = jnp.where(core == 0, second, first)
        q_keep[...] = keep[:, :HS]
        kv_keep[...] = keep[:, HS:]
        q_send[...] = send[:, :HS]
        kv_send[...] = send[:, HS:]

    return kernel


def attend(chips):
    bits = chips.bit_length() - 1

    def kernel(bounds, q_ids, key_ids, *refs):
        queries = refs[:2]
        same, other = refs[2 : 2 + chips], refs[2 + chips : 2 + 2 * chips]
        outs = refs[2 + 2 * chips : 4 + 2 * chips]
        kv, sem = refs[4 + 2 * chips :]
        chip, core, _ = place()
        copies = []
        for p in range(chips):
            source = 2 * chip_at(p, chip, core, bits)
            copies.append(pltpu.make_async_copy(same[p], kv.at[source + core], sem.at[2 * p]))
            copies.append(pltpu.make_async_copy(other[p], kv.at[source + 1 - core], sem.at[2 * p + 1]))
        for copy in copies:
            copy.start()
        for copy in copies:
            copy.wait()
        for t in range(2):
            q = queries[t][...]
            ids = q_ids[t]

            def step(block, carry):
                top, total, out = carry
                here = kv[block]
                scores = lax.dot_general(
                    q, here[:, :HS], (((1,), (1,)), ((), ())), preferred_element_type=F32
                ) * (HS**-0.5)
                scores = jnp.where(ids == key_ids[block], scores, NEG)
                new_top = jnp.maximum(top, jnp.max(scores, axis=1, keepdims=True))
                probs = jnp.exp(scores - new_top)
                fade = jnp.exp(top - new_top)
                total = total * fade + jnp.sum(probs, axis=1, keepdims=True)
                out = out * fade + jnp.dot(probs.astype(BF16), here[:, HS:], preferred_element_type=F32)
                return new_top, total, out

            rows = q.shape[0]
            start = (jnp.full((rows, 1), NEG, F32), jnp.zeros((rows, 1), F32), jnp.zeros((rows, HS), F32))
            _, total, out = lax.fori_loop(bounds[t, 0], bounds[t, 1], step, start)
            outs[t][...] = (out / total).astype(BF16)

    return kernel


def finish(chips, count):
    bits = chips.bit_length() - 1

    def kernel(*refs):
        mine, theirs = refs[:chips], refs[chips : 2 * chips]
        same, other = refs[2 * chips : 2 * chips + count], refs[2 * chips + count : 2 * chips + 2 * count]
        out, w_full, h_full, sem = refs[2 * chips + 2 * count :]
        chip, core, at = place()
        rows = mine[0].shape[0]
        copies = []

        def w_copy(block, source):
            to = w_full.at[pl.ds(pl.multiple_of(block * rows, rows), rows)]
            copies.append(pltpu.make_async_copy(source, to, sem.at[len(copies)]))

        def h_copy(block, source):
            to = h_full.at[:, pl.ds(pl.multiple_of(block * HS, HS), HS)]
            copies.append(pltpu.make_async_copy(source, to, sem.at[len(copies)]))

        for p in range(chips):
            w_copy(2 * chip_at(p, chip, core, bits) + core, mine[p])
            w_copy(2 * chip_at(p, chip, 1 - core, bits) + 1 - core, theirs[p])
        for k in range(count):
            source = lax.rem(at - k + count, count)
            h_copy(2 * source + core, same[k])
            h_copy(2 * source + 1 - core, other[k])
        for copy in copies:
            copy.start()
        for copy in copies:
            copy.wait()
        out[...] = jnp.dot(h_full[...], w_full[...], preferred_element_type=F32).astype(BF16)

    return kernel


def on_device(patches, segment_ids, w_query, w_key, w_value, w_out):
    rows, depth = patches.shape
    devices, count = lax.axis_size("seq"), lax.axis_size("tensor")
    chips = devices // 2
    width = w_query.shape[1]
    assert width == 2 * HS and devices == 2 * count and w_out.shape[0] == HS
    dma = pltpu.SemaphoreType.DMA
    shape = jax.ShapeDtypeStruct
    chip, core, at = place()

    below, above = line_gather(patches, count)

    w_all = jnp.concatenate(
        [w[:, h * HS : (h + 1) * HS] for h in range(2) for w in (w_query, w_key, w_value)], axis=1
    )
    w_mine = gather_chips(w_all, chips)
    w_theirs = [swap_cores(piece, devices) for piece in w_mine]

    ids = segment_ids.reshape(devices, rows)
    q_ids = jnp.stack([ids[2 * chip + core], ids[2 * chip + 1 - core]])
    low = jnp.sum(ids[None, :, -1] < q_ids[:, :1], axis=1)
    high = devices - jnp.sum(ids[None, :, 0] > q_ids[:, -1:], axis=1)
    bounds = jnp.stack([low, high], axis=1).astype(jnp.int32)

    steps = count - 2
    cols = 3 * width
    acc = pl.pallas_call(
        project_most(chips, count, steps),
        out_shape=shape((rows, cols), F32),
        in_specs=[ANY] * (2 * chips + 1 + 2 * steps),
        out_specs=VMEM,
        scratch_shapes=[
            pltpu.VMEM((count, rows, depth), BF16),
            pltpu.VMEM((count * depth, cols), BF16),
            dma((devices,)),
            dma((count,)),
        ],
        cost_estimate=pl.CostEstimate(
            flops=2 * rows * cols * depth * count,
            bytes_accessed=2 * count * depth * (rows + cols),
            transcendentals=0,
        ),
        name="project_most",
    )(*w_mine, *w_theirs, *below[: steps + 1], *above[1 : steps + 1])
    q_keep, kv_keep, q_send, kv_send = pl.pallas_call(
        project_last(chips, count),
        out_shape=[shape((rows, HS), BF16), shape((rows, 2 * HS), BF16)] * 2,
        in_specs=[ANY] * (2 * chips + 3),
        out_specs=[VMEM] * 4,
        scratch_shapes=[
            pltpu.VMEM((rows, cols), F32),
            pltpu.VMEM((rows, depth), BF16),
            pltpu.VMEM((depth, cols), BF16),
            dma((2,)),
            dma(()),
            dma(()),
        ],
        cost_estimate=pl.CostEstimate(
            flops=2 * rows * cols * depth,
            bytes_accessed=2 * depth * (rows + cols) + 4 * rows * cols,
            transcendentals=0,
        ),
        name="project_last",
    )(*w_mine, *w_theirs, acc, below[-1], above[-1])

    kv_same = gather_chips(kv_keep, chips)
    kv_other = gather_chips(swap_cores(kv_send, devices), chips)
    q_other = swap_cores(q_send, devices)

    h_keep, h_send = pl.pallas_call(
        attend(chips),
        out_shape=[shape((rows, HS), BF16)] * 2,
        in_specs=[SMEM, VMEM, VMEM, VMEM, VMEM] + [ANY] * (2 * chips),
        out_specs=[VMEM] * 2,
        scratch_shapes=[pltpu.VMEM((devices, rows, 2 * HS), BF16), dma((devices,))],
        cost_estimate=pl.CostEstimate(
            flops=8 * rows * rows * devices * HS,
            bytes_accessed=4 * rows * devices * HS,
            transcendentals=2 * rows * rows * devices,
        ),
        name="attend",
    )(bounds, q_ids[:, :, None], ids[:, None, :], q_keep, q_other, *kv_same, *kv_other)

    axes = ("seq", "tensor")
    h_same, h_other = [h_keep], []
    for k in range(count):
        for flip, source, into in ((0, h_keep, h_same), (1, h_send, h_other)):
            if k or flip:
                pairs = [
                    (s * count + z, (s ^ flip) * count + (z + k) % count)
                    for s in range(devices)
                    for z in range(count)
                ]
                into.append(lax.ppermute(source, axes, pairs))

    w_out_mine = gather_chips(w_out, chips)
    w_out_theirs = [swap_cores(piece, devices) for piece in w_out_mine]
    return pl.pallas_call(
        finish(chips, count),
        out_shape=shape((rows, w_out.shape[1]), BF16),
        in_specs=[ANY] * (2 * chips + 2 * count),
        out_specs=VMEM,
        scratch_shapes=[
            pltpu.VMEM((devices * HS, w_out.shape[1]), BF16),
            pltpu.VMEM((rows, devices * HS), BF16),
            dma((4 * chips,)),
        ],
        cost_estimate=pl.CostEstimate(
            flops=2 * rows * devices * HS * w_out.shape[1],
            bytes_accessed=2 * devices * HS * (rows + w_out.shape[1]),
            transcendentals=0,
        ),
        name="finish",
    )(*w_out_mine, *w_out_theirs, *h_same, *h_other)


def solution(mesh):
    spec = P("seq", "tensor")
    return jax.shard_map(
        on_device, mesh=mesh, in_specs=(spec, P(), spec, spec, spec, spec), out_specs=spec, check_vma=False
    )
```

```python
import jax
import jax.numpy as jnp
from jax import lax
from jax.experimental import pallas as pl
from jax.experimental.pallas import tpu as pltpu
from jax.sharding import PartitionSpec as P

HS = 128
NEG = -1e30
BF16 = jnp.bfloat16
F32 = jnp.float32
ANY = pl.BlockSpec(memory_space=pl.ANY)
VMEM = pl.BlockSpec(memory_space=pltpu.VMEM)
SMEM = pl.BlockSpec(memory_space=pltpu.SMEM)


def reversed_bits(value, bits):
    return sum(((value >> k) & 1) << (bits - 1 - k) for k in range(bits))


def chip_at(position, chip, core, bits):
    return chip ^ jnp.where(core == 0, position, reversed_bits(position, bits))


def permute(x, axes, pairs):
    return lax.ppermute(x, axes, pairs)


def gather_chips(x, chips):
    bits = chips.bit_length() - 1
    pieces = [x]
    for k in range(bits):
        pairs = [
            (2 * c + j, 2 * (c ^ (1 << (bits - 1 - k if j else k))) + j)
            for c in range(chips)
            for j in range(2)
        ]
        for q in range(1 << k):
            pieces.append(permute(pieces[q], "seq", pairs))
    return pieces


def swap_cores(pieces, devices):
    pairs = [(s, s ^ 1) for s in range(devices)]
    return [permute(piece, "seq", pairs) for piece in pieces]


def line_gather(x, count):
    below, above = [x], [x]
    for k in range(1, count):
        up = [(i, i + 1) for i in range(k - 1, count - 1)]
        down = [(i + 1, i) for i in range(count - k)]
        below.append(permute(below[-1], "tensor", up))
        above.append(permute(above[-1], "tensor", down))
    return below, above


def place():
    seq = lax.axis_index("seq")
    return seq // 2, seq % 2, lax.axis_index("tensor")


def project_most(chips, count, steps):
    bits = chips.bit_length() - 1

    def kernel(*refs):
        mine, theirs = refs[:chips], refs[chips : 2 * chips]
        xs = refs[2 * chips : 2 * chips + 1 + 2 * steps]
        acc, x_full, w_full, w_sem, x_sem = refs[2 * chips + 1 + 2 * steps :]
        chip, core, at = place()
        rows = mine[0].shape[0]

        def w_copy(block, source):
            to = w_full.at[pl.ds(pl.multiple_of(block * rows, rows), rows)]
            return pltpu.make_async_copy(source, to, w_sem.at[block])

        for p in range(chips):
            w_copy(2 * chip_at(p, chip, core, bits) + core, mine[p]).start()
            w_copy(2 * chip_at(p, chip, 1 - core, bits) + 1 - core, theirs[p]).start()

        def x_copy(block, source):
            return pltpu.make_async_copy(source, x_full.at[block], x_sem.at[block])

        x_copy(at, xs[0]).start()
        for k in range(1, steps + 1):

            @pl.when(at >= k)
            def _():
                x_copy(at - k, xs[k]).start()

            @pl.when(at + k < count)
            def _():
                x_copy(at + k, xs[steps + k]).start()

        acc[...] = jnp.zeros(acc.shape, F32)
        depth = x_full.shape[2]
        per = depth // rows

        def step(block, _):
            for i in range(per):
                w_copy(block * per + i, mine[0]).wait()

            @pl.when(jnp.abs(block - at) <= steps)
            def _():
                x_copy(block, xs[0]).wait()
                w = w_full[pl.ds(pl.multiple_of(block * depth, depth), depth), :]
                acc[...] += jnp.dot(x_full[block], w, preferred_element_type=F32)

            return 0

        lax.fori_loop(0, count, step, 0)

    return kernel


def project_last(chips, count):
    bits = chips.bit_length() - 1

    def kernel(*refs):
        mine, theirs = refs[:chips], refs[chips : 2 * chips]
        acc_in, from_below, from_above, q_out, kv_out = refs[2 * chips : 2 * chips + 5]
        acc, x_block, w_block, w_sem, x_sem, acc_sem = refs[2 * chips + 5 :]
        chip, core, at = place()
        rows = mine[0].shape[0]
        get_acc = pltpu.make_async_copy(acc_in, acc, acc_sem)
        get_acc.start()
        edge = (at == 0) | (at == count - 1)

        def w_copy(kind, source):
            return pltpu.make_async_copy(source, w_block.at[pl.ds(pl.multiple_of(kind * rows, rows), rows)], w_sem.at[kind])

        def x_copy(source):
            return pltpu.make_async_copy(source, x_block, x_sem)

        @pl.when(at == 0)
        def _():
            x_copy(from_above).start()

        @pl.when(at == count - 1)
        def _():
            x_copy(from_below).start()

        wanted = jnp.where(at == 0, count - 1, 0)
        for p in range(chips):

            @pl.when(edge & (chip_at(p, chip, core, bits) == wanted))
            def _():
                w_copy(core, mine[p]).start()

            @pl.when(edge & (chip_at(p, chip, 1 - core, bits) == wanted))
            def _():
                w_copy(1 - core, theirs[p]).start()

        get_acc.wait()

        @pl.when(edge)
        def _():
            x_copy(from_below).wait()
            w_copy(0, mine[0]).wait()
            w_copy(1, mine[0]).wait()
            acc[...] += jnp.dot(x_block[...], w_block[...], preferred_element_type=F32)

        width = q_out.shape[1]
        q_out[...] = acc[:, :width].astype(BF16)
        kv_out[...] = acc[:, width:].astype(BF16)

    return kernel


def attend(chips):
    bits = chips.bit_length() - 1

    def kernel(ids, key_ids, q_ref, *refs):
        mine, theirs = refs[:chips], refs[chips : 2 * chips]
        out_ref, kv, sem = refs[2 * chips :]
        chip, core, _ = place()
        copies = []
        for p in range(chips):
            source = 2 * chip_at(p, chip, core, bits) + core
            copies.append(pltpu.make_async_copy(mine[p], kv.at[source], sem.at[2 * p]))
            source = 2 * chip_at(p, chip, 1 - core, bits) + 1 - core
            copies.append(pltpu.make_async_copy(theirs[p], kv.at[source], sem.at[2 * p + 1]))
        for copy in copies:
            copy.start()
        rows, width = q_ref.shape
        own = 2 * chip + core
        first, last = ids[own * rows], ids[own * rows + rows - 1]

        def count_out(block, carry):
            low, high = carry
            low += (ids[block * rows + rows - 1] < first).astype(jnp.int32)
            high -= (ids[block * rows] > last).astype(jnp.int32)
            return low, high

        low, high = lax.fori_loop(0, 2 * chips, count_out, (0, 2 * chips))
        row_ids = jnp.broadcast_to(key_ids[own], (128, rows)).T[:, :1]
        queries = [q_ref[:, h * HS : (h + 1) * HS] for h in range(2)]
        for copy in copies:
            copy.wait()

        def step(block, carry):
            here = kv[block]
            same = row_ids == key_ids[block]
            result = []
            for h, (top, total, out) in enumerate(carry):
                keys = here[:, h * HS : (h + 1) * HS]
                values = here[:, width + h * HS : width + (h + 1) * HS]
                scores = lax.dot_general(
                    queries[h], keys, (((1,), (1,)), ((), ())), preferred_element_type=F32
                ) * (HS**-0.5)
                scores = jnp.where(same, scores, NEG)
                new_top = jnp.maximum(top, jnp.max(scores, axis=1, keepdims=True))
                probs = jnp.exp(scores - new_top)
                fade = jnp.exp(top - new_top)
                total = total * fade + jnp.sum(probs, axis=1, keepdims=True)
                out = out * fade + jnp.dot(probs.astype(BF16), values, preferred_element_type=F32)
                result.append((new_top, total, out))
            return tuple(result)

        start = (jnp.full((rows, 1), NEG, F32), jnp.zeros((rows, 1), F32), jnp.zeros((rows, HS), F32))
        for h, (_, total, out) in enumerate(lax.fori_loop(low, high, step, (start, start))):
            out_ref[:, h * HS : (h + 1) * HS] = (out / total).astype(BF16)

    return kernel


def finish(chips, count):
    bits = chips.bit_length() - 1

    def kernel(*refs):
        mine, theirs = refs[:chips], refs[chips : 2 * chips]
        heads = refs[2 * chips : 2 * chips + count]
        out, w_full, h_full, sem = refs[2 * chips + count :]
        chip, core, at = place()
        rows = mine[0].shape[0]
        width = heads[0].shape[1]
        copies = []

        def w_copy(block, source):
            to = w_full.at[pl.ds(pl.multiple_of(block * rows, rows), rows)]
            copies.append(pltpu.make_async_copy(source, to, sem.at[len(copies)]))

        for p in range(chips):
            w_copy(2 * chip_at(p, chip, core, bits) + core, mine[p])
            w_copy(2 * chip_at(p, chip, 1 - core, bits) + 1 - core, theirs[p])
        for k in range(count):
            source = lax.rem(at - k + count, count)
            to = h_full.at[:, pl.ds(pl.multiple_of(source * width, width), width)]
            copies.append(pltpu.make_async_copy(heads[k], to, sem.at[len(copies)]))
        for copy in copies:
            copy.start()
        for copy in copies:
            copy.wait()
        out[...] = jnp.dot(h_full[...], w_full[...], preferred_element_type=F32).astype(BF16)

    return kernel


def call(kernel, *args, flops, read, exps=0, **settings):
    cost = pl.CostEstimate(flops=flops, bytes_accessed=read, transcendentals=exps)
    return pl.pallas_call(kernel, cost_estimate=cost, **settings)(*args)


def steps_on_device(patches, segment_ids, w_query, w_key, w_value, w_out):
    rows, depth = patches.shape
    devices, count = lax.axis_size("seq"), lax.axis_size("tensor")
    chips = devices // 2
    width = w_query.shape[1]
    assert width == 2 * HS and devices == 2 * count and w_out.shape[0] == HS
    dma = pltpu.SemaphoreType.DMA
    shape = jax.ShapeDtypeStruct
    cols = 3 * width
    steps = count - 2

    below, above = line_gather(patches, count)
    w_mine = gather_chips(jnp.concatenate([w_query, w_key, w_value], axis=1), chips)
    w_theirs = swap_cores(w_mine, devices)
    out_mine = gather_chips(w_out, chips)
    out_theirs = swap_cores(out_mine, devices)

    acc = call(
        project_most(chips, count, steps),
        *w_mine,
        *w_theirs,
        *below[: steps + 1],
        *above[1 : steps + 1],
        flops=2 * rows * cols * depth * count,
        read=2 * count * depth * (rows + cols),
        out_shape=shape((rows, cols), F32),
        in_specs=[ANY] * (2 * chips + 1 + 2 * steps),
        out_specs=VMEM,
        scratch_shapes=[
            pltpu.VMEM((count, rows, depth), BF16),
            pltpu.VMEM((count * depth, cols), BF16),
            dma((devices,)),
            dma((count,)),
        ],
    )
    queries, kv = call(
        project_last(chips, count),
        *w_mine,
        *w_theirs,
        acc,
        below[-1],
        above[-1],
        flops=2 * rows * cols * depth,
        read=2 * depth * (rows + cols) + 4 * rows * cols,
        out_shape=[shape((rows, width), BF16), shape((rows, 2 * width), BF16)],
        in_specs=[ANY] * (2 * chips + 3),
        out_specs=[VMEM] * 2,
        scratch_shapes=[
            pltpu.VMEM((rows, cols), F32),
            pltpu.VMEM((rows, depth), BF16),
            pltpu.VMEM((depth, cols), BF16),
            dma((2,)),
            dma(()),
            dma(()),
        ],
    )

    kv_mine = gather_chips(kv, chips)
    kv_theirs = swap_cores(kv_mine, devices)
    heads = call(
        attend(chips),
        segment_ids,
        segment_ids.reshape(devices, 1, rows),
        queries,
        *kv_mine,
        *kv_theirs,
        flops=8 * rows * rows * devices * HS,
        read=8 * rows * devices * HS,
        exps=2 * rows * rows * devices,
        out_shape=shape((rows, width), BF16),
        in_specs=[SMEM, VMEM, VMEM] + [ANY] * (2 * chips),
        out_specs=VMEM,
        scratch_shapes=[pltpu.VMEM((devices, rows, 2 * width), BF16), dma((devices,))],
    )

    all_heads = [heads]
    for k in range(1, count):
        all_heads.append(permute(heads, "tensor", [(z, (z + k) % count) for z in range(count)]))
    return call(
        finish(chips, count),
        *out_mine,
        *out_theirs,
        *all_heads,
        flops=2 * rows * devices * HS * w_out.shape[1],
        read=2 * devices * HS * (rows + w_out.shape[1]),
        out_shape=shape((rows, w_out.shape[1]), BF16),
        in_specs=[ANY] * (2 * chips + count),
        out_specs=VMEM,
        scratch_shapes=[
            pltpu.VMEM((devices * HS, w_out.shape[1]), BF16),
            pltpu.VMEM((rows, devices * HS), BF16),
            dma((2 * chips + count,)),
        ],
    )


def solution(mesh):
    spec = P("seq", "tensor")
    return jax.shard_map(
        steps_on_device, mesh=mesh, in_specs=(spec, P(), spec, spec, spec, spec), out_specs=spec, check_vma=False
    )
```

```python
import jax
import jax.numpy as jnp
from jax import lax
from jax.experimental import pallas as pl
from jax.experimental.pallas import tpu as pltpu
from jax.sharding import PartitionSpec as P

HS = 128
NEG = -1e30
SPARE = 4 << 20
BF16 = jnp.bfloat16
F32 = jnp.float32
ANY = pl.BlockSpec(memory_space=pl.ANY)
VMEM = pl.BlockSpec(memory_space=pltpu.VMEM)
SMEM = pl.BlockSpec(memory_space=pltpu.SMEM)


def reversed_bits(value, bits):
    return sum(((value >> k) & 1) << (bits - 1 - k) for k in range(bits))


def chip_at(position, chip, core, bits):
    return chip ^ jnp.where(core == 0, position, reversed_bits(position, bits))


def permute(x, axes, pairs):
    return lax.ppermute(x, axes, pairs)


def gather_chips(x, chips):
    bits = chips.bit_length() - 1
    pieces = [x]
    for k in range(bits):
        pairs = [
            (2 * c + j, 2 * (c ^ (1 << (bits - 1 - k if j else k))) + j)
            for c in range(chips)
            for j in range(2)
        ]
        for q in range(1 << k):
            pieces.append(permute(pieces[q], "seq", pairs))
    return pieces


def swap_cores(pieces, devices):
    pairs = [(s, s ^ 1) for s in range(devices)]
    return [permute(piece, "seq", pairs) for piece in pieces]


def line_sources(step, chain, at):
    return (at + step + chain) % 2 == 0


def line_gather(x, count):
    chains = [[x], [x]]
    for k in range(1, count):
        for chain in (1, 0):
            pairs = []
            for i in range(count):
                up = line_sources(k, chain, i)
                if 0 <= (i - k if up else i + k) < count:
                    pairs.append((i - 1 if up else i + 1, i))
            if pairs:
                chains[chain].append(permute(chains[chain][-1], "tensor", pairs))
    return chains


def place():
    seq = lax.axis_index("seq")
    return seq // 2, seq % 2, lax.axis_index("tensor")


def project_most(chips, count, steps):
    bits = chips.bit_length() - 1

    def kernel(*refs):
        mine, theirs = refs[:chips], refs[chips : 2 * chips]
        xs = refs[2 * chips : 2 * chips + 1 + 2 * steps]
        acc, x_full, w_full, w_sem, x_sem = refs[2 * chips + 1 + 2 * steps :]
        chip, core, at = place()
        rows = mine[0].shape[0]

        def w_copy(block, source):
            to = w_full.at[pl.ds(pl.multiple_of(block * rows, rows), rows)]
            return pltpu.make_async_copy(source, to, w_sem.at[block])

        for p in range(chips):
            w_copy(2 * chip_at(p, chip, core, bits) + core, mine[p]).start()
            w_copy(2 * chip_at(p, chip, 1 - core, bits) + 1 - core, theirs[p]).start()

        def x_copy(block, source):
            return pltpu.make_async_copy(source, x_full.at[block], x_sem.at[block])

        x_copy(at, xs[0]).start()
        for k in range(1, steps + 1):
            for chain in range(2):
                block = jnp.where(line_sources(k, chain, at), at - k, at + k)

                @pl.when((block >= 0) & (block < count))
                def _():
                    x_copy(block, xs[chain * steps + k]).start()

        acc[...] = jnp.zeros(acc.shape, F32)
        depth = x_full.shape[2]
        per = depth // rows

        def step(block, _):
            for i in range(per):
                w_copy(block * per + i, mine[0]).wait()

            @pl.when(jnp.abs(block - at) <= steps)
            def _():
                x_copy(block, xs[0]).wait()
                w = w_full[pl.ds(pl.multiple_of(block * depth, depth), depth), :]
                acc[...] += jnp.dot(x_full[block], w, preferred_element_type=F32)

            return 0

        lax.fori_loop(0, count, step, 0)

    return kernel


def project_last(chips, count):
    bits = chips.bit_length() - 1

    def kernel(*refs):
        mine, theirs = refs[:chips], refs[chips : 2 * chips]
        acc_in, x_in, q_out, kv_out = refs[2 * chips : 2 * chips + 4]
        acc, x_block, w_block, w_sem, x_sem, acc_sem = refs[2 * chips + 4 :]
        chip, core, at = place()
        rows = mine[0].shape[0]
        get_acc = pltpu.make_async_copy(acc_in, acc, acc_sem)
        get_acc.start()
        edge = (at == 0) | (at == count - 1)

        def w_copy(kind, source):
            return pltpu.make_async_copy(source, w_block.at[pl.ds(pl.multiple_of(kind * rows, rows), rows)], w_sem.at[kind])

        x_copy = pltpu.make_async_copy(x_in, x_block, x_sem)

        @pl.when(edge)
        def _():
            x_copy.start()

        wanted = jnp.where(at == 0, count - 1, 0)
        for p in range(chips):

            @pl.when(edge & (chip_at(p, chip, core, bits) == wanted))
            def _():
                w_copy(core, mine[p]).start()

            @pl.when(edge & (chip_at(p, chip, 1 - core, bits) == wanted))
            def _():
                w_copy(1 - core, theirs[p]).start()

        get_acc.wait()

        @pl.when(edge)
        def _():
            x_copy.wait()
            w_copy(0, mine[0]).wait()
            w_copy(1, mine[0]).wait()
            acc[...] += jnp.dot(x_block[...], w_block[...], preferred_element_type=F32)

        width = q_out.shape[1]
        q_out[...] = acc[:, :width].astype(BF16)
        kv_out[...] = acc[:, width:].astype(BF16)

    return kernel


def attend(chips):
    bits = chips.bit_length() - 1

    def kernel(ids, key_ids, q_ref, *refs):
        mine, theirs = refs[:chips], refs[chips : 2 * chips]
        out_ref, kv, scores, sem = refs[2 * chips :]
        chip, core, _ = place()
        copies = []
        for p in range(chips):
            source = 2 * chip_at(p, chip, core, bits) + core
            copies.append(pltpu.make_async_copy(mine[p], kv.at[source], sem.at[2 * p]))
            source = 2 * chip_at(p, chip, 1 - core, bits) + 1 - core
            copies.append(pltpu.make_async_copy(theirs[p], kv.at[source], sem.at[2 * p + 1]))
        for copy in copies:
            copy.start()
        rows, width = q_ref.shape
        own = 2 * chip + core
        first, last = ids[own * rows], ids[own * rows + rows - 1]

        def count_out(block, carry):
            low, high = carry
            low += (ids[block * rows + rows - 1] < first).astype(jnp.int32)
            high -= (ids[block * rows] > last).astype(jnp.int32)
            return low, high

        low, high = lax.fori_loop(0, 2 * chips, count_out, (0, 2 * chips))
        row_ids = jnp.broadcast_to(key_ids[own], (128, rows)).T[:, :1]
        queries = [q_ref[:, h * HS : (h + 1) * HS] for h in range(2)]
        for copy in copies:
            copy.wait()

        lanes = [slice(i * HS, (i + 1) * HS) for i in range(rows // HS)]

        def score(block, tops):
            here = kv[block]
            same = row_ids == key_ids[block]
            result = []
            for h, top in enumerate(tops):
                keys = here[:, h * HS : (h + 1) * HS]
                dots = lax.dot_general(
                    queries[h], keys, (((1,), (1,)), ((), ())), preferred_element_type=F32
                )
                dots = jnp.where(same, dots, NEG)
                scores[h, block] = dots
                for lane in lanes:
                    top = jnp.maximum(top, dots[:, lane])
                result.append(top)
            return tuple(result)

        tops = lax.fori_loop(low, high, score, (jnp.full((rows, HS), NEG, F32),) * 2)
        tops = [jnp.max(top, axis=1, keepdims=True) for top in tops]

        def weigh(block, carry):
            here = kv[block]
            result = []
            for h, (total, out) in enumerate(carry):
                values = here[:, width + h * HS : width + (h + 1) * HS]
                probs = jnp.exp((scores[h, block] - tops[h]) * (HS**-0.5))
                for lane in lanes:
                    total = total + probs[:, lane]
                out = out + jnp.dot(probs.astype(BF16), values, preferred_element_type=F32)
                result.append((total, out))
            return tuple(result)

        zero = jnp.zeros((rows, HS), F32)
        for h, (total, out) in enumerate(lax.fori_loop(low, high, weigh, ((zero, zero),) * 2)):
            total = jnp.sum(total, axis=1, keepdims=True)
            out_ref[:, h * HS : (h + 1) * HS] = (out / total).astype(BF16)

    return kernel


def finish(chips, count):
    bits = chips.bit_length() - 1

    def kernel(*refs):
        mine, theirs = refs[:chips], refs[chips : 2 * chips]
        heads = refs[2 * chips : 2 * chips + count]
        out, w_full, h_full, sem = refs[2 * chips + count :]
        chip, core, at = place()
        rows = mine[0].shape[0]
        width = heads[0].shape[1]
        copies = []

        def w_copy(block, source):
            to = w_full.at[pl.ds(pl.multiple_of(block * rows, rows), rows)]
            copies.append(pltpu.make_async_copy(source, to, sem.at[len(copies)]))

        for p in range(chips):
            w_copy(2 * chip_at(p, chip, core, bits) + core, mine[p])
            w_copy(2 * chip_at(p, chip, 1 - core, bits) + 1 - core, theirs[p])
        for k in range(count):
            source = lax.rem(at - k + count, count)
            to = h_full.at[:, pl.ds(pl.multiple_of(source * width, width), width)]
            copies.append(pltpu.make_async_copy(heads[k], to, sem.at[len(copies)]))
        for copy in copies:
            copy.start()
        for copy in copies:
            copy.wait()
        out[...] = jnp.dot(h_full[...], w_full[...], preferred_element_type=F32).astype(BF16)

    return kernel


def call(kernel, *args, flops, read, vmem, exps=0, **settings):
    cost = pl.CostEstimate(flops=flops, bytes_accessed=read, transcendentals=exps)
    limit = pltpu.CompilerParams(vmem_limit_bytes=vmem)
    return pl.pallas_call(kernel, cost_estimate=cost, compiler_params=limit, **settings)(*args)


def steps_on_device(patches, segment_ids, w_query, w_key, w_value, w_out):
    rows, depth = patches.shape
    devices, count = lax.axis_size("seq"), lax.axis_size("tensor")
    chips = devices // 2
    width = w_query.shape[1]
    assert width == 2 * HS and devices == 2 * count and w_out.shape[0] == HS
    dma = pltpu.SemaphoreType.DMA
    shape = jax.ShapeDtypeStruct
    cols = 3 * width
    steps = count - 2

    chain0, chain1 = line_gather(patches, count)
    w_mine = gather_chips(jnp.concatenate([w_query, w_key, w_value], axis=1), chips)
    w_theirs = swap_cores(w_mine, devices)
    out_mine = gather_chips(w_out, chips)
    out_theirs = swap_cores(out_mine, devices)

    acc = call(
        project_most(chips, count, steps),
        *w_mine,
        *w_theirs,
        *chain0[: steps + 1],
        *chain1[1 : steps + 1],
        flops=2 * rows * cols * depth * count,
        read=2 * count * depth * (rows + cols),
        vmem=2 * count * depth * (rows + cols) + 8 * rows * cols + SPARE,
        out_shape=shape((rows, cols), F32),
        in_specs=[ANY] * (2 * chips + 1 + 2 * steps),
        out_specs=VMEM,
        scratch_shapes=[
            pltpu.VMEM((count, rows, depth), BF16),
            pltpu.VMEM((count * depth, cols), BF16),
            dma((devices,)),
            dma((count,)),
        ],
    )
    queries, kv = call(
        project_last(chips, count),
        *w_mine,
        *w_theirs,
        acc,
        chain0[-1],
        flops=2 * rows * cols * depth,
        read=2 * depth * (rows + cols) + 4 * rows * cols,
        vmem=2 * depth * (rows + cols) + 8 * rows * cols + SPARE,
        out_shape=[shape((rows, width), BF16), shape((rows, 2 * width), BF16)],
        in_specs=[ANY] * (2 * chips + 2),
        out_specs=[VMEM] * 2,
        scratch_shapes=[
            pltpu.VMEM((rows, cols), F32),
            pltpu.VMEM((rows, depth), BF16),
            pltpu.VMEM((depth, cols), BF16),
            dma((2,)),
            dma(()),
            dma(()),
        ],
    )

    kv_mine = gather_chips(kv, chips)
    kv_theirs = swap_cores(kv_mine, devices)
    heads = call(
        attend(chips),
        segment_ids,
        segment_ids.reshape(devices, 1, rows),
        queries,
        *kv_mine,
        *kv_theirs,
        flops=8 * rows * rows * devices * HS,
        read=8 * rows * devices * HS,
        exps=2 * rows * rows * devices,
        out_shape=shape((rows, width), BF16),
        in_specs=[SMEM, VMEM, VMEM] + [ANY] * (2 * chips),
        out_specs=VMEM,
        scratch_shapes=[
            pltpu.VMEM((devices, rows, 2 * width), BF16),
            pltpu.VMEM((2, devices, rows, rows), F32),
            dma((devices,)),
        ],
        vmem=devices * rows * (4 * width + 8 * rows) + SPARE,
    )

    all_heads = [heads]
    for k in range(1, count):
        all_heads.append(permute(heads, "tensor", [(z, (z + k) % count) for z in range(count)]))
    return call(
        finish(chips, count),
        *out_mine,
        *out_theirs,
        *all_heads,
        flops=2 * rows * devices * HS * w_out.shape[1],
        read=2 * devices * HS * (rows + w_out.shape[1]),
        vmem=2 * devices * HS * (rows + w_out.shape[1]) + 8 * rows * w_out.shape[1] + SPARE,
        out_shape=shape((rows, w_out.shape[1]), BF16),
        in_specs=[ANY] * (2 * chips + count),
        out_specs=VMEM,
        scratch_shapes=[
            pltpu.VMEM((devices * HS, w_out.shape[1]), BF16),
            pltpu.VMEM((rows, devices * HS), BF16),
            dma((2 * chips + count,)),
        ],
    )


def solution(mesh):
    spec = P("seq", "tensor")
    return jax.shard_map(
        steps_on_device, mesh=mesh, in_specs=(spec, P(), spec, spec, spec, spec), out_specs=spec, check_vma=False
    )
```
